128 devices in a mesh: gx: 8 (over y, core), gy: 16 (over z, x).
Axes of the slice: x: 4, y: 4, z: 4, core: 2. Of those that a mesh axis runs over, the one named last changes fastest.
Arguments:
- beta: float32 [16, 64, 2048], P(None, 'gx', 'gy'), may hold values from -6 to 6
- design: float32 [16, 16], replicated, may hold values from -1.5 to 1.5
- prior: float32 [16], replicated, may hold values from 0.25 to 4
- kept: int32 [16, 64, 2048], P(None, 'gx', 'gy'), may hold values from 1 to 40
- removed: int32 [16, 64, 2048], P(None, 'gx', 'gy'), may hold values from 0 to 8
- removed_labels: int32 [16, 64, 2048], P(None, 'gx', 'gy'), may hold values from 0 to 8, as said below
Outputs:
- newton_step: float32 [16, 64, 2048], P(None, 'gx', 'gy')
The draws below stay inside these ranges and needn't reach their ends.
Inputs may be any that keep to these rules, and one draw needn't show every extreme that they name: `removed_labels`: each entry is at most the entry of removed at the same place.
All inputs are finite; a program needn't handle non-finite values.
Results may differ from the reference program's by a relative error of at most 0.00022.
Values sent between devices are 32-bit elements; how exact they have to be, the bound alone decides.
A program may use at most 64 MiB of HBM per device.

```python
import math
import jax
import jax.numpy as jnp
from jax import lax

K = 16
J = 16
ITERS = 4
SWEEPS = 2
LEVELS = 4
COARSE_SWEEPS = 4
NX = 64
NY = 2048


def removal_pair(key):
    first = jax.random.fold_in(key, 11)
    second = jax.random.fold_in(key, 12)
    counts = jax.random.randint(first, (J, NX, NY), 0, 9, dtype=jnp.int32)
    labels = jax.random.randint(second, (J, NX, NY), 0, 9, dtype=jnp.int32) % (counts + 1)
    return (counts, labels)


def draw_removed(key, part):
    return removal_pair(key)[0]


def draw_removed_labels(key, part):
    return removal_pair(key)[1]


def touch_ends(array, key, smallest, largest):
    extent = array.shape
    place = [jax.random.randint(jax.random.fold_in(key, axis), (), 0, extent[axis]) for axis in range(len(extent))]
    array = array.at[tuple(place)].set(smallest)
    longest = extent.index(max(extent))
    place[longest] = (place[longest] + 1) % extent[longest]
    return array.at[tuple(place)].set(largest)


def level_of(stream_key, dims, split, least, top_value):
    def one(position, blocks):
        steps = jax.random.uniform(jax.random.fold_in(jax.random.fold_in(stream_key, 6), position), (blocks,), jnp.float32, least / len(split), top_value / len(split))
        return jnp.repeat(jnp.exp(steps), dims[position] // blocks).reshape((-1,) + (1,) * (len(dims) - position - 1))

    gain = one(*split[0])
    for cut in split[1:]:
        gain = gain * one(*cut)
    return gain


def normal_values(own_key, dims, deviation, bound, shards=(), held_as=jnp.bfloat16):
    gain = level_of(own_key, dims, shards, -0.22, 0.18) if shards else 1.0
    values = jax.random.normal(own_key, dims, jnp.float32) * deviation * gain
    return jnp.minimum(jnp.maximum(values, -bound), bound).astype(held_as)


def setup_inputs(seed: int = 0) -> dict:
    keys = jax.random.split(jax.random.key(seed), 7)
    beta = normal_values(keys[0], (K, NX, NY), 1.0, 6.0, ((1, 8), (2, 16)), jnp.float32)
    design = normal_values(keys[1], (J, K), K ** -0.5, 1.5, (), jnp.float32)
    prior = jnp.clip(jnp.exp(jax.random.uniform(keys[2], (K,), jnp.float32, math.log(0.25), math.log(4.0))), 0.25, 4.0)
    kept = touch_ends(jax.random.randint(keys[3], (J, NX, NY), 1, 41), jax.random.fold_in(keys[3], 1), 1, 40).astype(jnp.int32)
    removed = draw_removed(jax.random.fold_in(keys[6], 71), 0)
    removed_labels = draw_removed_labels(jax.random.fold_in(keys[6], 71), 0)
    return {"beta": beta, "design": design, "prior": prior, "kept": kept, "removed": removed, "removed_labels": removed_labels}


damping = 0.7
highest = lax.Precision.HIGHEST


def gauss_jordan(blocks):
    size = blocks.shape[0]
    for pivot_at in range(size):
        pivots = blocks[pivot_at, pivot_at]
        scaled = blocks[pivot_at].at[pivot_at].set(1.0) / pivots[None]
        factors = blocks[:, pivot_at]
        blocks = blocks.at[:, pivot_at].set(0.0) - factors[:, None] * scaled[None]
        blocks = blocks.at[pivot_at].set(scaled)
    return blocks


def apply_inverse(inverse, vector):
    return jnp.einsum("klxy,lxy->kxy", inverse, vector, precision=highest)


def operate(field, padded, design, weights, prior, scale):
    inner = jnp.einsum("jk,kxy->jxy", design, field, precision=highest)
    data_term = jnp.einsum("jk,jxy->kxy", design, weights * inner, precision=highest)
    beside = padded[:, 2:, 1:-1] + padded[:, :-2, 1:-1] + padded[:, 1:-1, 2:] + padded[:, 1:-1, :-2]
    return data_term + scale * prior[:, None, None] * (4.0 * field - beside)


def restrict(field):
    chans, rows, cols = field.shape
    return field.reshape(chans, rows // 2, 2, cols // 2, 2).sum(axis=(2, 4))


def prolong(field):
    return jnp.repeat(jnp.repeat(field, 2, axis=1), 2, axis=2)


def build_inverse(design, weights, prior, scale):
    outer = design[:, :, None] * design[:, None, :]
    blocks = jnp.einsum("jkl,jxy->klxy", outer, weights, precision=highest)
    blocks = blocks + (4.0 * scale * jnp.diag(prior))[:, :, None, None]
    return gauss_jordan(blocks)


def zero_pad(field):
    return jnp.pad(field, ((0, 0), (1, 1), (1, 1)))


def smooth(field, rhs, design, weights, inverse, prior, scale):
    leftover = rhs - operate(field, zero_pad(field), design, weights, prior, scale)
    return field + damping * apply_inverse(inverse, leftover)


def sweeps(rhs, count, design, weights, inverse, prior, scale):
    field = damping * apply_inverse(inverse, rhs)
    for sweep in range(count - 1):
        field = smooth(field, rhs, design, weights, inverse, prior, scale)
    return field


def multigrid(rhs, level, tables, design, prior):
    weights, inverse = tables[level]
    scale = 2.0 ** level
    if level == len(tables) - 1:
        return sweeps(rhs, COARSE_SWEEPS, design, weights, inverse, prior, scale)
    field = sweeps(rhs, SWEEPS, design, weights, inverse, prior, scale)
    leftover = rhs - operate(field, zero_pad(field), design, weights, prior, scale)
    field = field + prolong(multigrid(restrict(leftover), level + 1, tables, design, prior))
    for sweep in range(SWEEPS):
        field = smooth(field, rhs, design, weights, inverse, prior, scale)
    return field


def reference(beta, design, prior, kept, removed, removed_labels):
    logits = jnp.einsum("jk,kxy->jxy", design, beta, precision=highest)
    prob = 1.0 / (1.0 + jnp.exp(-logits))
    weights = kept.astype(jnp.float32) * prob * (1.0 - prob)
    source = removed.astype(jnp.float32) * prob - removed_labels.astype(jnp.float32)
    rhs = jnp.einsum("jk,jxy->kxy", design, source, precision=highest)
    tables = []
    for level in range(LEVELS):
        if level > 0:
            weights = restrict(weights)
        tables.append((weights, build_inverse(design, weights, prior, 2.0 ** level)))
    fine_weights = tables[0][0]
    newton_step = jnp.zeros_like(rhs)
    residual = rhs
    precond = multigrid(residual, 0, tables, design, prior)
    direction = precond
    gamma = jnp.sum(residual * precond)
    for step in range(ITERS):
        image = operate(direction, zero_pad(direction), design, fine_weights, prior, 1.0)
        alpha = gamma / jnp.sum(direction * image)
        newton_step = newton_step + alpha * direction
        residual = residual - alpha * image
        if step + 1 < ITERS:
            precond = multigrid(residual, 0, tables, design, prior)
            gamma_next = jnp.sum(residual * precond)
            direction = precond + (gamma_next / gamma) * direction
            gamma = gamma_next
    return newton_step
```

```python
import jax
import jax.numpy as jnp
from jax import lax
from jax.experimental import pallas as pl
from jax.experimental.pallas import tpu as pltpu
from jax.sharding import PartitionSpec as P

K = 16
ITERS = 4
NTILES = 7
GX, GY = 8, 16
damping = 0.7
keep = 1.0 - damping
MESH = pl.DeviceIdType.MESH
F32 = jnp.float32

level_tiles = {0: (0, 1, 2), 1: (3, 4), 2: (5,), 3: (6,)}
tile_level = (0, 0, 0, 1, 1, 2, 3)
around = ((-1, -1), (-1, 0), (-1, 1), (0, -1), (0, 1), (1, -1), (1, 0), (1, 1))
sideways = tuple(o for o in around if o[1] != 0)


def iota(axis):
    return lax.broadcasted_iota(jnp.int32, (8, 128), axis)


def take(x, index, axis):
    return jnp.take_along_axis(x, index, axis=axis, mode="promise_in_bounds")


def lroll(x, shift):
    return pltpu.roll(x, shift % 128, x.ndim - 1)


def sroll(x, shift):
    return pltpu.roll(x, shift % 8, x.ndim - 2)


def body(
    beta, design, prior, kept, removed, labels, out,
    dv, pv, mask, nat, wt, a, mi, mb,
    fb, d1, d2, rho, v,
    zs, qs, ss, ds, xs, rs, us, ws, scal,
    tw, tf, pw, pf, psw, psf, g1b, g2b, s1w, s1f, s2w, s2f, r1w, r1f, r2w, r2f,
    lsend, lgx, lgy, lsum,
    e0s, e0r, e1s, e1r, e2s, e2r, ags, agr, bgs, bgr,
):
    mx, my = lax.axis_index("gx"), lax.axis_index("gy")
    sub, lane = iota(0), iota(1)

    def device(dx, dy):
        return (lax.rem(mx + dx + GX, GX), lax.rem(my + dy + GY, GY))

    barrier = pltpu.get_barrier_semaphore()
    peers = [(d, 0) for d in range(1, GX)] + [(0, d) for d in range(1, GY)]
    peers += [o for o in around if o[0] != 0 and o[1] != 0]
    for dx, dy in peers:
        pl.semaphore_signal(barrier, inc=1, device_id=device(dx, dy), device_id_type=MESH)

    def remote(src, dst, ssem, rsem, dx, dy):
        return pltpu.make_async_remote_copy(
            src_ref=src, dst_ref=dst, send_sem=ssem, recv_sem=rsem, device_id=device(dx, dy), device_id_type=MESH
        )

    def copies0(t, p, ps, k):
        out = [
            remote(t.at[pl.ds(0, 64)], t.at[pl.ds(128, 64)], e0s.at[k, 0], e0r.at[k, 0], -1, 0),
            remote(t.at[pl.ds(64, 64)], t.at[pl.ds(192, 64)], e0s.at[k, 1], e0r.at[k, 1], 1, 0),
        ]
        for j, (dx, dy) in enumerate(sideways):
            slot = sideways.index((-dx, -dy))
            out.append(remote(ps, p.at[slot], e0s.at[k, 2 + j], e0r.at[k, 2 + j], dx, dy))
        return out

    group = (lane + 4) // 8 % 16
    right_side = lane % 8 < 4
    even_half = (lane < 32) | (lane >= 96)

    def pack(rows_of, ps):
        total = jnp.zeros((8, 128), F32)
        for c in range(K):
            x = rows_of(c)
            total = jnp.where(group == c, lroll(x, 8 * c), total)
        ps[...] = total

    def load0(t, p, dst):
        def merged(dx):
            return jnp.where(right_side, p[sideways.index((dx, 1))], p[sideways.index((dx, -1))])

        here, below, above = merged(0), merged(1), merged(-1)
        even = jnp.where(sub < 4, here, sroll(jnp.where(sub < 2, below, above), 4))
        odd = jnp.where(sub < 4, sroll(here, 4), jnp.where(sub < 6, below, above))
        for c in range(K):
            dst[0, pl.ds(8 * c, 8), :] = t[pl.ds(c, 8, stride=32), :]
            dst[1, pl.ds(8 * c, 8), :] = t[pl.ds(16 + c, 8, stride=32), :]
            dst[2, pl.ds(8 * c, 8), :] = jnp.where(even_half, lroll(even, -8 * c), lroll(odd, 64 - 8 * c))

    def natural_start(src, t, p, ps, k):
        for r in range(8):
            t[pl.ds(16 * r, 16), :] = src[pl.ds(r, 16, stride=8), :]
        pack(lambda c: jnp.concatenate([src[pl.ds(8 * c + i, 4, stride=2), :] for i in range(2)], axis=0), ps)
        for copy in copies0(t, p, ps, k):
            copy.start()

    lane_even = lane % 2 == 0
    split = jnp.where(lane < 64, 2 * lane, 2 * (lane - 64) + 1)

    def restrict_pairs(src, first, g):
        for c in range(8):
            lo = src[first, pl.ds(8 * c, 8), :] + src[first + 1, pl.ds(8 * c, 8), :]
            hi = src[first, pl.ds(8 * c + 64, 8), :] + src[first + 1, pl.ds(8 * c + 64, 8), :]
            g[pl.ds(8 * c, 8), :] = take(jnp.where(lane_even, lo + lroll(lo, -1), hi + lroll(hi, 1)), split, 1)

    def copies1(s, r, k):
        rows = {1: (0, 40, 88), -1: (8, 40, 32), 0: (8, 32, 0)}
        out = []
        for j, (dx, dy) in enumerate(around):
            start, size, target = rows[dx]
            out.append(
                remote(s.at[pl.ds(start, size)], r.at[1 - dy, pl.ds(target, size)], e1s.at[k, j], e1r.at[k, j], dx, dy)
            )
        return out

    def start1(src, s, r, k):
        restrict_pairs(src, 0, g1b)
        s[pl.ds(0, 8), :] = g1b[pl.ds(7, 8, stride=8), :]
        for i in range(5):
            s[pl.ds(8 + 8 * i, 8), :] = g1b[pl.ds(i, 8, stride=8), :]
        for copy in copies1(s, r, k):
            copy.start()
        r[1, pl.ds(0, 32), :] = s[pl.ds(8, 32), :]

    middle = (lane >= 32) & (lane < 96)
    from_left = (lane // 32) % 2 == 1

    def load1(r, dst):
        for tile, base in ((3, 0), (4, 8)):
            for c in range(8):
                left, here, right = (r[g, pl.ds(base + c, 8, stride=16), :] for g in range(3))
                side = jnp.where(from_left, left, right)
                dst[tile, pl.ds(8 * c, 8), :] = jnp.where(middle, lroll(here, 32), lroll(side, 96))
                dst[tile, pl.ds(8 * c + 64, 8), :] = jnp.where(middle, lroll(here, 96), lroll(side, 32))

    def copies2(s, r, k):
        return [
            remote(s, r.at[pl.ds(16 * (GX - d), 16)], e2s.at[k, d - 1], e2r.at[k, d - 1], d, 0) for d in range(1, GX)
        ]

    def start2(src, s, r, k):
        restrict_pairs(src, 3, g2b)
        s[pl.ds(0, 8), :] = g2b[pl.ds(0, 8, stride=8), :]
        s[pl.ds(8, 8), :] = g2b[pl.ds(1, 8, stride=8), :]
        for copy in copies2(s, r, k):
            copy.start()
        r[pl.ds(0, 16), :] = s[...]

    def load2(r, dst):
        for c in range(8):
            even, odd = r[pl.ds(c, 8, stride=16), :], r[pl.ds(8 + c, 8, stride=16), :]
            dst[5, pl.ds(8 * c, 8), :] = jnp.where(lane < 64, even, lroll(odd, 64))
            dst[5, pl.ds(8 * c + 64, 8), :] = jnp.where(lane < 64, lroll(even, 64), odd)

    def finish(copies):
        for copy in copies:
            copy.wait_recv()
        for copy in copies:
            copy.wait_send()

    twice = 2 * lane % 64

    def restrict3(src, dst):
        for c in range(K):
            x = src[5, pl.ds(8 * c, 8), :]
            x = x + lroll(x, 64)
            dst[6, pl.ds(8 * c, 8), :] = take(x + lroll(x, -1), twice, 1)

    def fill(j, carry):
        for k in range(K):
            dv[j, k] = jnp.full((8, 128), design[j, k], F32)
        return carry

    lax.fori_loop(0, K, fill, 0)
    for t in range(NTILES):
        for k in range(K):
            pv[t, pl.ds(8 * k, 8), :] = jnp.full((8, 128), prior[k] * 2.0 ** tile_level[t], F32)

    def one(condition):
        return jnp.where(condition, 1.0, 0.0).astype(F32)

    for t in range(2):
        row = jnp.where(sub < 6, 2 * sub, 2 * sub - 16) + t
        at = 8 * mx + row
        mask[t] = one((at >= 0) & (at < 64))
    row = jnp.where(sub < 6, 2 * sub, 2 * sub - 16) + jnp.where(even_half, 0, 1)
    at = 8 * mx + row
    offset = (lane + 32) % 64 - 32
    column = 128 * my + jnp.where(offset < 0, offset, 128 + offset)
    mask[2] = one((at >= 0) & (at < 64) & (offset >= -4) & (offset < 4) & (column >= 0) & (column < 2048))
    for t in range(2):
        row = jnp.where(sub < 5, 2 * sub, 2 * sub - 16) + t
        at = 4 * mx + row
        column = lane - 32
        near = (row >= -5) & (row <= 8) & (column >= -26) & (column < 90)
        column = 64 * my + column
        mask[3 + t] = one(near & (at >= 0) & (at < 32) & (column >= 0) & (column < 1024))
    column = lane % 64 - 16
    near = (column >= -12) & (column < 44)
    column = 32 * my + column
    mask[5] = one(near & (column >= 0) & (column < 512))
    column = lane - 8
    near = (column >= -5) & (column < 21)
    column = 16 * my + column
    mask[6] = one(near & (column >= 0) & (column < 256))
    at = lax.rem(mx + sub, GX)
    first, last = at == 0, at == GX - 1
    mask[7] = one(~(((lane < 64) & first) | ((lane >= 64) & last)))
    mask[8] = one(~first)
    mask[9] = one(~last)

    logits = dv[:, 0] * beta[0]
    for k in range(1, K):
        logits = logits + dv[:, k] * beta[k]
    prob = 1.0 / (1.0 + jnp.exp(-logits))
    nat[0] = (kept[...].astype(F32) * prob * (1.0 - prob)).reshape(128, 128)
    nat[1] = (removed[...].astype(F32) * prob - labels[...].astype(F32)).reshape(128, 128)
    total = dv[0] * nat[1, pl.ds(0, 8), :]
    for j in range(1, K):
        total = total + dv[j] * nat[1, pl.ds(8 * j, 8), :]
    nat[1] = total.reshape(128, 128)

    for r in (r1w, r1f):
        r[...] = jnp.zeros_like(r)

    pl.semaphore_wait(barrier, len(peers))
    natural_start(nat.at[0], tw, pw, psw, 0)
    natural_start(nat.at[1], tf, pf, psf, 1)

    zero = jnp.zeros((2, 128, 128), F32)
    for ref in (zs, qs, ss, ds, xs, us, ws):
        ref[...] = zero
    rest = jnp.zeros((4, 128), F32)
    for t in range(2):
        for c in range(K):
            rs[t, pl.ds(8 * c, 8), :] = jnp.concatenate([nat[1, pl.ds(8 * c + t, 4, stride=2), :], rest], axis=0)

    def weight(t, j):
        return jnp.where(mask[t] > 0.0, wt[t, pl.ds(pl.multiple_of(8 * j, 8), 8), :], 0.0)

    def invert(t, fine):
        w = [weight(t, j) for j in range(K)]
        for k in range(K):
            total = (dv[0, k] * w[0]) * dv[0, : k + 1]
            for j in range(1, K):
                total = total + (dv[j, k] * w[j]) * dv[j, : k + 1]
            a[k, : k + 1] = total
            a[k, k] = a[k, k] + 4.0 * pv[t, pl.ds(8 * k, 8), :]
            if fine:
                mb[t, k, : k + 1] = a[k, : k + 1]
                if k:
                    mb[t, :k, k] = a[k, :k]

        def line(i):
            if i == K - 1:
                return a[i, : i + 1]
            return jnp.concatenate([a[i, : i + 1], a[i + 1 :, i]], axis=0)

        def put(i, value):
            a[i, : i + 1] = value[: i + 1]
            if i < K - 1:
                a[i + 1 :, i] = value[i + 1 :]

        def replaced(value, i, entry):
            parts = [value[:i], entry[None], value[i + 1 :]]
            return jnp.concatenate([part for part in parts if part.shape[0]], axis=0)

        for p in range(0, K, 2):
            q = p + 1
            col1 = line(p)
            inv1 = 1.0 / col1[p]
            sc1 = col1 * inv1
            col2 = replaced(line(q) - sc1[q] * col1, p, sc1[q])
            inv2 = 1.0 / col2[q]
            sc2 = col2 * inv2
            for i in range(K):
                if i not in (p, q):
                    a[i, : i + 1] = a[i, : i + 1] - sc1[i] * col1[: i + 1] - sc2[i] * col2[: i + 1]
            line_p = replaced(sc1 - sc2[p] * col2, p, -inv1 - sc2[p] * col2[p])
            put(p, replaced(line_p, q, sc2[p]))
            put(q, replaced(sc2, q, -inv2))
        factor = -damping * mask[t]
        for i in range(K):
            value = a[i, : i + 1] * factor
            mi[t, i, : i + 1] = value
            if i:
                mi[t, :i, i] = value[:i]

    def invert_tiles(first, stop, fine):
        def step(t, carry):
            invert(t, fine)
            return carry

        lax.fori_loop(first, stop, step, 0)

    finish(copies0(tw, pw, psw, 0))
    load0(tw, pw, wt)
    start1(wt, s1w, r1w, 0)
    invert_tiles(0, 2, True)
    finish(copies1(s1w, r1w, 0))
    load1(r1w, wt)
    start2(wt, s2w, r2w, 2)
    invert_tiles(2, 5, False)
    finish(copies2(s2w, r2w, 2))
    load2(r2w, wt)
    restrict3(wt, wt)
    invert_tiles(5, 7, False)

    def product(matrix, t, src):
        total = matrix[t, 0] * src[t, pl.ds(0, 8), :]
        for l in range(1, K):
            total = total + matrix[t, l] * src[t, pl.ds(8 * l, 8), :]
        return total.reshape(128, 128)

    STEP = 4

    def beside(level, src, g):
        def get(t):
            return src[t, pl.ds(8 * STEP * g, 8 * STEP), :].reshape(STEP, 8, 128)

        def pick(condition, x, y):
            return jnp.where(condition[None], x, y)

        if level == 0:
            e, o, h = get(0), get(1), get(2)
            y = lroll(h, 64)
            e1, o1, h1, y1 = lroll(e, 1), lroll(o, 1), lroll(h, 1), lroll(y, 1)
            em, om, hm, ym = lroll(e, -1), lroll(o, -1), lroll(h, -1), lroll(y, -1)
            start, end = lane == 0, lane == 127
            ne = o + sroll(o, 1) + pick(start, h1, e1) + pick(end, hm, em)
            no = e + sroll(e, -1) + pick(start, y1, o1) + pick(end, ym, om)
            nh = y + pick(even_half, sroll(y, 1), sroll(y, -1))
            nh = nh + pick(start, e1, pick(lane == 64, lroll(o1, 64), h1))
            nh = nh + pick(end, em, pick(lane == 63, lroll(om, 64), hm))
            return ne, no, nh
        if level == 1:
            e, o = get(3), get(4)
            ne = o + sroll(o, 1) + lroll(e, 1) + lroll(e, -1)
            no = e + sroll(e, -1) + lroll(o, 1) + lroll(o, -1)
            return ne, no
        if level == 2:
            x = get(5)
            y = lroll(x, 64)
            n = y + mask[7][None] * pick(lane < 64, sroll(y, 1), sroll(y, -1))
            return (n + lroll(x, 1) + lroll(x, -1),)
        x = get(6)
        return (mask[8][None] * sroll(x, 1) + mask[9][None] * sroll(x, -1) + lroll(x, 1) + lroll(x, -1),)

    def stencil(level, src, combine):
        for g in range(K // STEP):
            rows = pl.ds(8 * STEP * g, 8 * STEP)
            for t, n in zip(level_tiles[level], beside(level, src, g)):
                rho[t, rows, :] = combine(t, rows, pv[t, rows, :] * n.reshape(8 * STEP, 128))

    def descend(level):
        for t in level_tiles[level]:
            d1[t] = product(mi, t, fb)
        stencil(level, d1, lambda t, rows, n: keep * fb[t, rows, :] + n)
        for t in level_tiles[level]:
            value = product(mi, t, rho)
            d2[t] = value
            v[t] = d1[t] + value
        stencil(level, d2, lambda t, rows, n: keep * rho[t, rows, :] + n)

    def smooth(level, count):
        def step(i, carry):
            stencil(level, v, lambda t, rows, n: fb[t, rows, :] + n)
            for t in level_tiles[level]:
                v[t] = keep * v[t] + product(mi, t, rho)
            return carry

        lax.fori_loop(0, count, step, 0)

    up_rows = jnp.where(sub < 6, sub // 2, 7)
    up3 = lane % 64 // 2
    up2 = lane // 2 + 64 * (sub % 2)
    up1 = lane // 2 + 32
    beside_lane = jnp.where(offset < 0, (offset + 4) // 2 + 30, offset // 2 + 96)
    up1_side = jnp.where((offset >= -4) & (offset < 4), beside_lane, 0)
    sub_even = sub % 2 == 0

    def cycle(wait_first, k):
        descend(0)
        start1(rho, s1f, r1f, 1)
        wait_first()
        finish(copies1(s1f, r1f, 1))
        load1(r1f, fb)
        descend(1)
        parity = lax.rem(k, 2)
        start2(rho, s2f, r2f.at[parity], parity)
        finish(copies2(s2f, r2f.at[parity], parity))
        load2(r2f.at[parity], fb)
        descend(2)
        restrict3(rho, fb)
        v[6] = product(mi, 6, fb)
        smooth(3, 3)
        for c in range(K):
            rows = pl.ds(8 * c, 8)
            v[5, rows, :] = v[5, rows, :] + take(v[6, rows, :], up3, 1)
        smooth(2, 2)
        for c in range(K):
            rows = pl.ds(8 * c, 8)
            e = take(take(v[5, rows, :], up_rows, 0), up2, 1)
            for t in (3, 4):
                v[t, rows, :] = v[t, rows, :] + mask[t] * e
        smooth(1, 2)
        for c in range(K):
            rows = pl.ds(8 * c, 8)
            e = jnp.where(sub_even, take(v[3, rows, :], up_rows, 0), take(v[4, rows, :], up_rows, 0))
            main = take(e, up1, 1)
            v[0, rows, :] = v[0, rows, :] + main
            v[1, rows, :] = v[1, rows, :] + main
            v[2, rows, :] = v[2, rows, :] + take(e, up1_side, 1)
        smooth(0, 2)

    def copies_a(k):
        return [remote(lsend, lgx.at[k, GX - d], ags.at[k, d - 1], agr.at[k, d - 1], d, 0) for d in range(1, GX)]

    def copies_b(k):
        return [remote(lsum, lgy.at[k, GY - d], bgs.at[k, d - 1], bgr.at[k, d - 1], 0, d) for d in range(1, GY)]

    def dot(x, y):
        total = jnp.zeros((8, 128), F32)
        for t in range(2):
            for c in range(K):
                rows = pl.ds(8 * c, 8)
                total = total + x[t, rows, :] * y[t, rows, :]
        total = jnp.sum(jnp.where(sub < 4, total, 0.0), axis=0, keepdims=True)
        return jnp.sum(total, axis=1, keepdims=True)

    one_lane = lax.broadcasted_iota(jnp.int32, (1, 128), 1)

    def sum_start(k):
        gamma, delta, cross = dot(rs, us), dot(ws, us), dot(ss, us)
        lsend[...] = jnp.where(one_lane == 0, gamma, jnp.where(one_lane == 1, delta, cross))
        for copy in copies_a(k):
            copy.start()
        lgx[k, 0] = lsend[...]

    def sum_turn(k):
        finish(copies_a(k))
        total = lgx[k, 0]
        for i in range(1, GX):
            total = total + lgx[k, i]
        lsum[...] = total
        for copy in copies_b(k):
            copy.start()
        lgy[k, 0] = total

    def sum_finish(k, use_beta):
        finish(copies_b(k))
        total = lgy[k, 0]
        for i in range(1, GY):
            total = total + lgy[k, i]

        def lane_of(i):
            value = jnp.sum(jnp.where(one_lane == i, total, 0.0), axis=1, keepdims=True)
            return jnp.broadcast_to(value, (8, 128))

        gamma, delta, cross = lane_of(0), lane_of(1), lane_of(2)
        beta_now = use_beta * gamma / scal[2]
        product_now = delta + 2.0 * beta_now * cross + beta_now * beta_now * scal[3]
        scal[0] = gamma / product_now
        scal[1] = beta_now
        scal[2] = gamma
        scal[3] = product_now

    scal[0] = jnp.full((8, 128), -1.0, F32)
    scal[1] = jnp.zeros((8, 128), F32)
    scal[2] = jnp.ones((8, 128), F32)
    scal[3] = jnp.zeros((8, 128), F32)

    def trip(k, carry):
        finish(copies0(tf, pf, psf, 1))
        load0(tf, pf, fb)
        before = lax.rem(k + 1, 2)

        def turn():
            @pl.when(k > 0)
            def _():
                sum_turn(before)

        cycle(turn, k)
        stencil(0, v, lambda t, rows, n: n)
        for t in range(2):
            d1[t] = product(mb, t, v) - rho[t]

        @pl.when(k > 0)
        def _():
            sum_finish(before, jnp.where(k > 1, 1.0, 0.0))

        def update(new, old, ref, sum_ref, t, rows):
            turned = new + scal[1] * old
            ref[t, rows, :] = turned
            return turned

        for t in range(2):
            for c in range(K):
                rows = pl.ds(8 * c, 8)
                z = d1[t, rows, :] + scal[1] * zs[t, rows, :]
                zs[t, rows, :] = z
                old = ws[t, rows, :]
                ss[t, rows, :] = old + scal[1] * ss[t, rows, :]
                ws[t, rows, :] = old - scal[0] * z

        @pl.when(k < ITERS - 1)
        def _():
            for i in range(4):
                tf[pl.ds(32 * i, 16), :] = ws[0, pl.ds(i, 16, stride=8), :]
                tf[pl.ds(32 * i + 16, 16), :] = ws[1, pl.ds(i, 16, stride=8), :]
            pack(lambda c: jnp.where(sub < 4, ws[0, pl.ds(8 * c, 8), :], sroll(ws[1, pl.ds(8 * c, 8), :], 4)), psf)
            for copy in copies0(tf, pf, psf, 1):
                copy.start()

        for t in range(2):
            for c in range(K):
                rows = pl.ds(8 * c, 8)
                q = v[t, rows, :] + scal[1] * qs[t, rows, :]
                qs[t, rows, :] = q
                old = us[t, rows, :]
                d = old + scal[1] * ds[t, rows, :]
                ds[t, rows, :] = d
                xs[t, rows, :] = xs[t, rows, :] + scal[0] * d
                rs[t, rows, :] = rs[t, rows, :] - scal[0] * ss[t, rows, :]
                us[t, rows, :] = old - scal[0] * q
        sum_start(lax.rem(k, 2))
        return carry

    lax.fori_loop(0, ITERS, trip, 0)
    last_k = (ITERS - 1) % 2
    sum_turn(last_k)
    sum_finish(last_k, 1.0)
    for t in range(2):
        for c in range(K):
            rows = pl.ds(8 * c, 8)
            d = us[t, rows, :] + scal[1] * ds[t, rows, :]
            xs[t, rows, :] = xs[t, rows, :] + scal[0] * d
    for i in range(4):
        tf[pl.ds(32 * i, 16), :] = xs[0, pl.ds(i, 16, stride=8), :]
        tf[pl.ds(32 * i + 16, 16), :] = xs[1, pl.ds(i, 16, stride=8), :]
    for c in range(K):
        out[c] = tf[pl.ds(c, 8, stride=16), :]


def local(beta, design, prior, kept, removed, removed_labels):
    def vmem(*shape):
        return pltpu.VMEM(shape, F32)

    def dma(*shape):
        return pltpu.SemaphoreType.DMA(shape)

    whole = pl.BlockSpec(memory_space=pltpu.VMEM)
    scalars = pl.BlockSpec(memory_space=pltpu.SMEM)
    field = (NTILES, 128, 128)
    pair = (2, 128, 128)
    return pl.pallas_call(
        body,
        out_shape=jax.ShapeDtypeStruct(beta.shape, F32),
        in_specs=[whole, scalars, scalars, whole, whole, whole],
        out_specs=whole,
        scratch_shapes=[
            vmem(K, K, 8, 128), vmem(*field), vmem(10, 8, 128), vmem(*pair), vmem(*field),
            vmem(K, K, 8, 128), vmem(NTILES, K, K, 8, 128), vmem(2, K, K, 8, 128),
            *[vmem(*field) for _ in range(5)],
            *[vmem(*pair) for _ in range(8)], vmem(4, 8, 128),
            vmem(256, 128), vmem(256, 128), vmem(6, 8, 128), vmem(6, 8, 128), vmem(8, 128), vmem(8, 128),
            vmem(64, 128), vmem(64, 128), vmem(48, 128), vmem(48, 128), vmem(16, 128), vmem(16, 128),
            vmem(3, 128, 128), vmem(3, 128, 128), vmem(128, 128), vmem(2, 128, 128),
            vmem(1, 128), vmem(2, GX, 1, 128), vmem(2, GY, 1, 128), vmem(1, 128),
            dma(2, 8), dma(2, 8), dma(2, 8), dma(2, 8), dma(3, 7), dma(3, 7),
            dma(2, GX - 1), dma(2, GX - 1), dma(2, GY - 1), dma(2, GY - 1),
        ],
        compiler_params=pltpu.CompilerParams(collective_id=0, has_side_effects=True, vmem_limit_bytes=48 << 20),
    )(beta, design, prior, kept, removed, removed_labels)


def solution(mesh):
    placed = (
        P(None, "gx", "gy"),
        P(),
        P(),
        P(None, "gx", "gy"),
        P(None, "gx", "gy"),
        P(None, "gx", "gy"),
    )
    return jax.shard_map(
        local, mesh=mesh, in_specs=placed, out_specs=P(None, "gx", "gy"), check_vma=False
    )
```

```python
import jax
import jax.numpy as jnp
from jax import lax
from jax.experimental import pallas as pl
from jax.experimental.pallas import tpu as pltpu
from jax.sharding import PartitionSpec as P

K = 16
ITERS = 4
NTILES = 7
GX, GY = 8, 16
damping = 0.7
keep = 1.0 - damping
MESH = pl.DeviceIdType.MESH
F32 = jnp.float32

level_tiles = {0: (0, 1, 2), 1: (3, 4), 2: (5,), 3: (6,)}
tile_level = (0, 0, 0, 1, 1, 2, 3)
around = ((-1, -1), (-1, 0), (-1, 1), (0, -1), (0, 1), (1, -1), (1, 0), (1, 1))
sideways = tuple(o for o in around if o[1] != 0)


def iota(axis):
    return lax.broadcasted_iota(jnp.int32, (8, 128), axis)


def take(x, index, axis):
    return jnp.take_along_axis(x, index, axis=axis, mode="promise_in_bounds")


def lroll(x, shift):
    return pltpu.roll(x, shift % 128, x.ndim - 1)


def sroll(x, shift):
    return pltpu.roll(x, shift % 8, x.ndim - 2)


def body(
    beta_in, design_in, prior_in, kept_in, removed_in, labels_in, out,
    beta, design, prior, kept, removed, labels, insem, dv, pv, mask, nat, wt, a, mi, mb,
    fb, d1, d2, rho, v,
    zs, qs, ss, ds, xs, rs, us, ws, scal,
    tw, tf, pw, pf, psw, psf, g1b, g2b, s1w, s1f, s2w, s2f, r1w, r1f, r2w, r2f,
    lsend, lgx, lgy, lsum, lall,
    e0s, e0r, e1s, e1r, e2s, e2r, ags, agr, bgs, bgr, alls, allr,
):
    mx, my = lax.axis_index("gx"), lax.axis_index("gy")
    sub, lane = iota(0), iota(1)

    def device(dx, dy):
        return (lax.rem(mx + dx + GX, GX), lax.rem(my + dy + GY, GY))

    inputs = [
        pltpu.make_async_copy(src, dst, insem.at[i])
        for i, (src, dst) in enumerate(
            (
                (design_in, design), (prior_in, prior), (beta_in, beta),
                (kept_in, kept), (removed_in, removed), (labels_in, labels),
            )
        )
    ]
    for copy in inputs:
        copy.start()

    for r in (r1w, r1f, pw, pf):
        r[...] = jnp.zeros_like(r)
    for t in (tw, tf):
        t[pl.ds(128, 128), :] = jnp.zeros((128, 128), F32)

    barrier = pltpu.get_barrier_semaphore()
    peers = [(d, 0) for d in range(1, GX)] + [(0, d) for d in range(1, GY)]
    peers += [o for o in around if o[0] != 0 and o[1] != 0]
    for dx, dy in peers:
        pl.semaphore_signal(barrier, inc=1, device_id=device(dx, dy), device_id_type=MESH)

    has = {-1: mx > 0, 1: mx < GX - 1}
    has_y = {-1: my > 0, 1: my < GY - 1}

    def exists(dx, dy):
        found = [table[d] for table, d in ((has, dx), (has_y, dy)) if d]
        return found[0] if len(found) == 1 else found[0] & found[1]

    def remote(src, dst, ssem, rsem, dx, dy):
        return pltpu.make_async_remote_copy(
            src_ref=src, dst_ref=dst, send_sem=ssem, recv_sem=rsem, device_id=device(dx, dy), device_id_type=MESH
        )

    def copies0(t, p, ps, k):
        out = []
        for j, (dx, dy) in enumerate(sideways):
            slot = sideways.index((-dx, -dy))
            out.append((remote(ps, p.at[slot], e0s.at[k, 2 + j], e0r.at[k, 2 + j], dx, dy), dx, dy))
        out.append((remote(t.at[pl.ds(0, 64)], t.at[pl.ds(128, 64)], e0s.at[k, 0], e0r.at[k, 0], -1, 0), -1, 0))
        out.append((remote(t.at[pl.ds(64, 64)], t.at[pl.ds(192, 64)], e0s.at[k, 1], e0r.at[k, 1], 1, 0), 1, 0))
        return out

    def start(copies):
        for copy, dx, dy in copies:
            pl.when(exists(dx, dy))(copy.start)

    def finish(copies):
        for copy, dx, dy in copies:
            pl.when(exists(-dx, -dy))(copy.wait_recv)
        for copy, dx, dy in copies:
            pl.when(exists(dx, dy))(copy.wait_send)

    def finish_all(copy):
        copy.wait_recv()
        copy.wait_send()

    group = (lane + 4) // 8 % 16
    right_side = lane % 8 < 4
    even_half = (lane < 32) | (lane >= 96)

    def pack(rows_of, ps):
        total = jnp.zeros((8, 128), F32)
        for c in range(K):
            x = rows_of(c)
            total = jnp.where(group == c, lroll(x, 8 * c), total)
        ps[...] = total

    def load0(t, p, dst):
        def merged(dx):
            return jnp.where(right_side, p[sideways.index((dx, 1))], p[sideways.index((dx, -1))])

        here, below, above = merged(0), merged(1), merged(-1)
        even = jnp.where(sub < 4, here, sroll(jnp.where(sub < 2, below, above), 4))
        odd = jnp.where(sub < 4, sroll(here, 4), jnp.where(sub < 6, below, above))
        for c in range(K):
            dst[0, pl.ds(8 * c, 8), :] = t[pl.ds(c, 8, stride=32), :]
            dst[1, pl.ds(8 * c, 8), :] = t[pl.ds(16 + c, 8, stride=32), :]
            dst[2, pl.ds(8 * c, 8), :] = jnp.where(even_half, lroll(even, -8 * c), lroll(odd, 64 - 8 * c))

    def natural_start(src, t, p, ps, k):
        for r in range(8):
            t[pl.ds(16 * r, 16), :] = src[pl.ds(r, 16, stride=8), :]
        pack(lambda c: jnp.concatenate([src[pl.ds(8 * c + i, 4, stride=2), :] for i in range(2)], axis=0), ps)
        start(copies0(t, p, ps, k))

    lane_even = lane % 2 == 0
    split = jnp.where(lane < 64, 2 * lane, 2 * (lane - 64) + 1)

    def restrict_pairs(src, first, g):
        for c in range(8):
            lo = src[first, pl.ds(8 * c, 8), :] + src[first + 1, pl.ds(8 * c, 8), :]
            hi = src[first, pl.ds(8 * c + 64, 8), :] + src[first + 1, pl.ds(8 * c + 64, 8), :]
            g[pl.ds(8 * c, 8), :] = take(jnp.where(lane_even, lo + lroll(lo, -1), hi + lroll(hi, 1)), split, 1)

    def copies1(s, r, k):
        rows = {1: (0, 40, 88), -1: (8, 40, 32), 0: (8, 32, 0)}
        out = []
        for j, (dx, dy) in enumerate(around):
            first, size, target = rows[dx]
            src, dst = s.at[pl.ds(first, size)], r.at[1 - dy, pl.ds(target, size)]
            out.append((remote(src, dst, e1s.at[k, j], e1r.at[k, j], dx, dy), dx, dy))
        return out

    def start1(src, s, r, k):
        restrict_pairs(src, 0, g1b)
        s[pl.ds(0, 8), :] = g1b[pl.ds(7, 8, stride=8), :]
        for i in range(5):
            s[pl.ds(8 + 8 * i, 8), :] = g1b[pl.ds(i, 8, stride=8), :]
        start(copies1(s, r, k))
        r[1, pl.ds(0, 32), :] = s[pl.ds(8, 32), :]

    middle = (lane >= 32) & (lane < 96)
    from_left = (lane // 32) % 2 == 1

    def load1(r, dst):
        for tile, base in ((3, 0), (4, 8)):
            for c in range(8):
                left, here, right = (r[g, pl.ds(base + c, 8, stride=16), :] for g in range(3))
                side = jnp.where(from_left, left, right)
                dst[tile, pl.ds(8 * c, 8), :] = jnp.where(middle, lroll(here, 32), lroll(side, 96))
                dst[tile, pl.ds(8 * c + 64, 8), :] = jnp.where(middle, lroll(here, 96), lroll(side, 32))

    def copies2(s, r, k):
        return [
            remote(s, r.at[pl.ds(16 * (GX - d), 16)], e2s.at[k], e2r.at[k], d, 0) for d in range(1, GX)
        ]

    def finish2(r, k):
        rest = r.at[pl.ds(16, 16 * (GX - 1))]
        finish_all(remote(rest, rest, e2s.at[k], e2r.at[k], 1, 0))

    def start2(src, s, r, k):
        restrict_pairs(src, 3, g2b)
        s[pl.ds(0, 8), :] = g2b[pl.ds(0, 8, stride=8), :]
        s[pl.ds(8, 8), :] = g2b[pl.ds(1, 8, stride=8), :]
        for copy in copies2(s, r, k):
            copy.start()
        r[pl.ds(0, 16), :] = s[...]

    def load2(r, dst):
        for c in range(8):
            even, odd = r[pl.ds(c, 8, stride=16), :], r[pl.ds(8 + c, 8, stride=16), :]
            dst[5, pl.ds(8 * c, 8), :] = jnp.where(lane < 64, even, lroll(odd, 64))
            dst[5, pl.ds(8 * c + 64, 8), :] = jnp.where(lane < 64, lroll(even, 64), odd)

    twice = 2 * lane % 64

    def restrict3(src, dst):
        for c in range(K):
            x = src[5, pl.ds(8 * c, 8), :]
            x = x + lroll(x, 64)
            dst[6, pl.ds(8 * c, 8), :] = take(x + lroll(x, -1), twice, 1)

    def one(condition):
        return jnp.where(condition, 1.0, 0.0).astype(F32)

    for t in range(2):
        row = jnp.where(sub < 6, 2 * sub, 2 * sub - 16) + t
        at = 8 * mx + row
        mask[t] = one((at >= 0) & (at < 64))
    row = jnp.where(sub < 6, 2 * sub, 2 * sub - 16) + jnp.where(even_half, 0, 1)
    at = 8 * mx + row
    offset = (lane + 32) % 64 - 32
    column = 128 * my + jnp.where(offset < 0, offset, 128 + offset)
    mask[2] = one((at >= 0) & (at < 64) & (offset >= -4) & (offset < 4) & (column >= 0) & (column < 2048))
    for t in range(2):
        row = jnp.where(sub < 5, 2 * sub, 2 * sub - 16) + t
        at = 4 * mx + row
        column = lane - 32
        near = (row >= -5) & (row <= 8) & (column >= -26) & (column < 90)
        column = 64 * my + column
        mask[3 + t] = one(near & (at >= 0) & (at < 32) & (column >= 0) & (column < 1024))
    column = lane % 64 - 16
    near = (column >= -12) & (column < 44)
    column = 32 * my + column
    mask[5] = one(near & (column >= 0) & (column < 512))
    column = lane - 8
    near = (column >= -5) & (column < 21)
    column = 16 * my + column
    mask[6] = one(near & (column >= 0) & (column < 256))
    at = lax.rem(mx + sub, GX)
    first, last = at == 0, at == GX - 1
    mask[7] = one(~(((lane < 64) & first) | ((lane >= 64) & last)))
    mask[8] = one(~first)
    mask[9] = one(~last)

    for copy in inputs:
        copy.wait()

    def fill(j, carry):
        for k in range(K):
            dv[j, k] = jnp.full((8, 128), design[j, k], F32)
        return carry

    lax.fori_loop(0, K, fill, 0)
    for t in range(NTILES):
        for k in range(K):
            pv[t, pl.ds(8 * k, 8), :] = jnp.full((8, 128), prior[k] * 2.0 ** tile_level[t], F32)

    logits = dv[:, 0] * beta[0]
    for k in range(1, K):
        logits = logits + dv[:, k] * beta[k]
    prob = 1.0 / (1.0 + jnp.exp(-logits))
    nat[0] = (kept[...].astype(F32) * prob * (1.0 - prob)).reshape(128, 128)
    nat[1] = (removed[...].astype(F32) * prob - labels[...].astype(F32)).reshape(128, 128)
    total = dv[0] * nat[1, pl.ds(0, 8), :]
    for j in range(1, K):
        total = total + dv[j] * nat[1, pl.ds(8 * j, 8), :]
    nat[1] = total.reshape(128, 128)


    pl.semaphore_wait(barrier, len(peers))
    natural_start(nat.at[0], tw, pw, psw, 0)
    natural_start(nat.at[1], tf, pf, psf, 1)

    zero = jnp.zeros((2, 128, 128), F32)
    for ref in (zs, qs, ss, ds, xs, us, ws):
        ref[...] = zero
    rest = jnp.zeros((4, 128), F32)
    for t in range(2):
        for c in range(K):
            rs[t, pl.ds(8 * c, 8), :] = jnp.concatenate([nat[1, pl.ds(8 * c + t, 4, stride=2), :], rest], axis=0)

    def weight(t, j):
        return jnp.where(mask[t] > 0.0, wt[t, pl.ds(pl.multiple_of(8 * j, 8), 8), :], 0.0)

    def invert(t):
        w = [weight(t, j) for j in range(K)]
        for k in range(K):
            total = (dv[0, k] * w[0]) * dv[0, : k + 1]
            for j in range(1, K):
                total = total + (dv[j, k] * w[j]) * dv[j, : k + 1]
            a[k, : k + 1] = total
            a[k, k] = a[k, k] + 4.0 * pv[t, pl.ds(8 * k, 8), :]

        @pl.when(t < 2)
        def _():
            for k in range(K):
                mb[t, k, : k + 1] = a[k, : k + 1]
                if k:
                    mb[t, :k, k] = a[k, :k]

        def line(i):
            if i == K - 1:
                return a[i, : i + 1]
            return jnp.concatenate([a[i, : i + 1], a[i + 1 :, i]], axis=0)

        def put(i, value):
            a[i, : i + 1] = value[: i + 1]
            if i < K - 1:
                a[i + 1 :, i] = value[i + 1 :]

        def replaced(value, i, entry):
            parts = [value[:i], entry[None], value[i + 1 :]]
            return jnp.concatenate([part for part in parts if part.shape[0]], axis=0)

        for p in range(0, K, 2):
            q = p + 1
            col1 = line(p)
            inv1 = 1.0 / col1[p]
            sc1 = col1 * inv1
            col2 = replaced(line(q) - sc1[q] * col1, p, sc1[q])
            inv2 = 1.0 / col2[q]
            sc2 = col2 * inv2
            for i in range(K):
                if i not in (p, q):
                    a[i, : i + 1] = a[i, : i + 1] - sc1[i] * col1[: i + 1] - sc2[i] * col2[: i + 1]
            line_p = replaced(sc1 - sc2[p] * col2, p, -inv1 - sc2[p] * col2[p])
            put(p, replaced(line_p, q, sc2[p]))
            put(q, replaced(sc2, q, -inv2))
        factor = -damping * mask[t]
        for i in range(K):
            value = a[i, : i + 1] * factor
            mi[t, i, : i + 1] = value
            if i:
                mi[t, :i, i] = value[:i]

    def invert_tiles(first, stop):
        def step(t, carry):
            invert(t)
            return carry

        lax.fori_loop(first, stop, step, 0)

    finish(copies0(tw, pw, psw, 0))
    load0(tw, pw, wt)
    start1(wt, s1w, r1w, 0)
    invert_tiles(0, 3)
    finish(copies1(s1w, r1w, 0))
    load1(r1w, wt)
    start2(wt, s2w, r2w, 2)

    def product(matrix, t, src):
        total = matrix[t, 0] * src[t, pl.ds(0, 8), :]
        for l in range(1, K):
            total = total + matrix[t, l] * src[t, pl.ds(8 * l, 8), :]
        return total.reshape(128, 128)

    STEP = 4

    def beside(level, src, g):
        def get(t):
            return src[t, pl.ds(8 * STEP * g, 8 * STEP), :].reshape(STEP, 8, 128)

        def pick(condition, x, y):
            return jnp.where(condition[None], x, y)

        if level == 0:
            e, o, h = get(0), get(1), get(2)
            y = lroll(h, 64)
            e1, o1, h1, y1 = lroll(e, 1), lroll(o, 1), lroll(h, 1), lroll(y, 1)
            em, om, hm, ym = lroll(e, -1), lroll(o, -1), lroll(h, -1), lroll(y, -1)
            start, end = lane == 0, lane == 127
            ne = o + sroll(o, 1) + pick(start, h1, e1) + pick(end, hm, em)
            no = e + sroll(e, -1) + pick(start, y1, o1) + pick(end, ym, om)
            nh = y + pick(even_half, sroll(y, 1), sroll(y, -1))
            nh = nh + pick(start, e1, pick(lane == 64, lroll(o1, 64), h1))
            nh = nh + pick(end, em, pick(lane == 63, lroll(om, 64), hm))
            return ne, no, nh
        if level == 1:
            e, o = get(3), get(4)
            ne = o + sroll(o, 1) + lroll(e, 1) + lroll(e, -1)
            no = e + sroll(e, -1) + lroll(o, 1) + lroll(o, -1)
            return ne, no
        if level == 2:
            x = get(5)
            y = lroll(x, 64)
            n = y + mask[7][None] * pick(lane < 64, sroll(y, 1), sroll(y, -1))
            return (n + lroll(x, 1) + lroll(x, -1),)
        x = get(6)
        return (mask[8][None] * sroll(x, 1) + mask[9][None] * sroll(x, -1) + lroll(x, 1) + lroll(x, -1),)

    def stencil(level, src, combine):
        for g in range(K // STEP):
            rows = pl.ds(8 * STEP * g, 8 * STEP)
            for t, n in zip(level_tiles[level], beside(level, src, g)):
                rho[t, rows, :] = combine(t, rows, pv[t, rows, :] * n.reshape(8 * STEP, 128))

    def descend(level):
        for t in level_tiles[level]:
            d1[t] = product(mi, t, fb)
        stencil(level, d1, lambda t, rows, n: keep * fb[t, rows, :] + n)
        for t in level_tiles[level]:
            value = product(mi, t, rho)
            d2[t] = value
            v[t] = d1[t] + value
        stencil(level, d2, lambda t, rows, n: keep * rho[t, rows, :] + n)

    def smooth(level, count):
        def step(i, carry):
            stencil(level, v, lambda t, rows, n: fb[t, rows, :] + n)
            for t in level_tiles[level]:
                v[t] = keep * v[t] + product(mi, t, rho)
            return carry

        lax.fori_loop(0, count, step, 0)

    up_rows = jnp.where(sub < 6, sub // 2, 7)
    up3 = lane % 64 // 2
    up2 = lane // 2 + 64 * (sub % 2)
    up1 = lane // 2 + 32
    beside_lane = jnp.where(offset < 0, (offset + 4) // 2 + 30, offset // 2 + 96)
    up1_side = jnp.where((offset >= -4) & (offset < 4), beside_lane, 0)
    sub_even = sub % 2 == 0

    def cycle(wait_first, wait_second, k):
        descend(0)
        start1(rho, s1f, r1f, 1)
        wait_first()
        finish(copies1(s1f, r1f, 1))
        load1(r1f, fb)
        descend(1)
        parity = lax.rem(k, 2)
        start2(rho, s2f, r2f.at[parity], parity)
        wait_second()
        finish2(r2f.at[parity], parity)
        load2(r2f.at[parity], fb)
        descend(2)
        restrict3(rho, fb)
        v[6] = product(mi, 6, fb)
        smooth(3, 3)
        for c in range(K):
            rows = pl.ds(8 * c, 8)
            v[5, rows, :] = v[5, rows, :] + take(v[6, rows, :], up3, 1)
        smooth(2, 2)
        for c in range(K):
            rows = pl.ds(8 * c, 8)
            e = take(take(v[5, rows, :], up_rows, 0), up2, 1)
            for t in (3, 4):
                v[t, rows, :] = v[t, rows, :] + mask[t] * e
        smooth(1, 2)
        for c in range(K):
            rows = pl.ds(8 * c, 8)
            e = jnp.where(sub_even, take(v[3, rows, :], up_rows, 0), take(v[4, rows, :], up_rows, 0))
            main = take(e, up1, 1)
            v[0, rows, :] = v[0, rows, :] + main
            v[1, rows, :] = v[1, rows, :] + main
            v[2, rows, :] = v[2, rows, :] + take(e, up1_side, 1)
        smooth(0, 2)

    def copies_a(k):
        return [remote(lsend, lgx.at[k, GX - d], ags.at[k], agr.at[k], d, 0) for d in range(1, GX)]

    def copies_b(k):
        return [remote(lsum, lgy.at[k, GY - d], bgs.at[k], bgr.at[k], 0, d) for d in range(1, GY)]

    def finish_sum(landing, count, ssem, rsem):
        rest = landing.at[pl.ds(1, count - 1)]
        finish_all(remote(rest, rest, ssem, rsem, 0, 1))

    def dot(x, y):
        total = jnp.zeros((8, 128), F32)
        for t in range(2):
            for c in range(K):
                rows = pl.ds(8 * c, 8)
                total = total + x[t, rows, :] * y[t, rows, :]
        total = jnp.sum(jnp.where(sub < 4, total, 0.0), axis=0, keepdims=True)
        return jnp.sum(total, axis=1, keepdims=True)

    one_lane = lax.broadcasted_iota(jnp.int32, (1, 128), 1)

    def sum_parts():
        gamma, delta, cross = dot(rs, us), dot(ws, us), dot(ss, us)
        lsend[...] = jnp.where(one_lane == 0, gamma, jnp.where(one_lane == 1, delta, cross))

    def sum_start(k):
        sum_parts()
        for copy in copies_a(k):
            copy.start()
        lgx[k, 0] = lsend[...]

    def sum_turn(k):
        finish_sum(lgx.at[k], GX, ags.at[k], agr.at[k])
        total = lgx[k, 0]
        for i in range(1, GX):
            total = total + lgx[k, i]
        lsum[...] = total
        for copy in copies_b(k):
            copy.start()
        lgy[k, 0] = total

    def sum_finish(k, use_beta):
        finish_sum(lgy.at[k], GY, bgs.at[k], bgr.at[k])
        scalars(jnp.sum(lgy[k], axis=0), use_beta)

    def sum_at_once():
        sum_parts()
        for d in range(1, GX * GY):
            dx, dy = d // GY, d % GY
            slot = (GX - dx) % GX * GY + (GY - dy) % GY
            remote(lsend, lall.at[slot], alls, allr, dx, dy).start()
        lall[0] = lsend[...]
        finish_sum(lall, GX * GY, alls, allr)
        scalars(jnp.sum(lall[...], axis=0), 1.0)

    def scalars(total, use_beta):

        def lane_of(i):
            value = jnp.sum(jnp.where(one_lane == i, total, 0.0), axis=1, keepdims=True)
            return jnp.broadcast_to(value, (8, 128))

        gamma, delta, cross = lane_of(0), lane_of(1), lane_of(2)
        beta_now = use_beta * gamma / scal[2]
        product_now = delta + 2.0 * beta_now * cross + beta_now * beta_now * scal[3]
        scal[0] = gamma / product_now
        scal[1] = beta_now
        scal[2] = gamma
        scal[3] = product_now

    scal[0] = jnp.full((8, 128), -1.0, F32)
    scal[1] = jnp.zeros((8, 128), F32)
    scal[2] = jnp.ones((8, 128), F32)
    scal[3] = jnp.zeros((8, 128), F32)

    def trip(k, carry):
        finish(copies0(tf, pf, psf, 1))
        load0(tf, pf, fb)
        before = lax.rem(k + 1, 2)

        def turn():
            @pl.when(k > 0)
            def _():
                sum_turn(before)

            @pl.when(k == 0)
            def _():
                invert_tiles(3, 5)
                finish2(r2w, 2)
                load2(r2w, wt)
                restrict3(wt, wt)

        def coarse():
            @pl.when(k == 0)
            def _():
                invert_tiles(5, 7)

        cycle(turn, coarse, k)
        stencil(0, v, lambda t, rows, n: n)
        for t in range(2):
            d1[t] = product(mb, t, v) - rho[t]

        @pl.when(k > 0)
        def _():
            sum_finish(before, jnp.where(k > 1, 1.0, 0.0))

        def update(new, old, ref, sum_ref, t, rows):
            turned = new + scal[1] * old
            ref[t, rows, :] = turned
            return turned

        for t in range(2):
            for c in range(K):
                rows = pl.ds(8 * c, 8)
                z = d1[t, rows, :] + scal[1] * zs[t, rows, :]
                zs[t, rows, :] = z
                old = ws[t, rows, :]
                ss[t, rows, :] = old + scal[1] * ss[t, rows, :]
                ws[t, rows, :] = old - scal[0] * z

        @pl.when(k < ITERS - 1)
        def _():
            for i in range(4):
                tf[pl.ds(32 * i, 16), :] = ws[0, pl.ds(i, 16, stride=8), :]
                tf[pl.ds(32 * i + 16, 16), :] = ws[1, pl.ds(i, 16, stride=8), :]
            pack(lambda c: jnp.where(sub < 4, ws[0, pl.ds(8 * c, 8), :], sroll(ws[1, pl.ds(8 * c, 8), :], 4)), psf)
            start(copies0(tf, pf, psf, 1))

        for t in range(2):
            for c in range(K):
                rows = pl.ds(8 * c, 8)
                q = v[t, rows, :] + scal[1] * qs[t, rows, :]
                qs[t, rows, :] = q
                old = us[t, rows, :]
                d = old + scal[1] * ds[t, rows, :]
                ds[t, rows, :] = d
                xs[t, rows, :] = xs[t, rows, :] + scal[0] * d
                rs[t, rows, :] = rs[t, rows, :] - scal[0] * ss[t, rows, :]
                us[t, rows, :] = old - scal[0] * q

        @pl.when(k < ITERS - 1)
        def _():
            sum_start(lax.rem(k, 2))

        return carry

    lax.fori_loop(0, ITERS, trip, 0)
    sum_at_once()
    for t in range(2):
        for c in range(K):
            rows = pl.ds(8 * c, 8)
            d = us[t, rows, :] + scal[1] * ds[t, rows, :]
            xs[t, rows, :] = xs[t, rows, :] + scal[0] * d
    for i in range(4):
        tf[pl.ds(32 * i, 16), :] = xs[0, pl.ds(i, 16, stride=8), :]
        tf[pl.ds(32 * i + 16, 16), :] = xs[1, pl.ds(i, 16, stride=8), :]
    for c in range(K):
        out[c] = tf[pl.ds(c, 8, stride=16), :]


def local(beta, design, prior, kept, removed, removed_labels):
    def vmem(*shape):
        return pltpu.VMEM(shape, F32)

    def dma(*shape):
        return pltpu.SemaphoreType.DMA(shape)

    whole = pl.BlockSpec(memory_space=pltpu.VMEM)
    outside = pl.BlockSpec(memory_space=pltpu.HBM)
    counts = pltpu.VMEM((K, 8, 128), jnp.int32)
    field = (NTILES, 128, 128)
    pair = (2, 128, 128)
    return pl.pallas_call(
        body,
        out_shape=jax.ShapeDtypeStruct(beta.shape, F32),
        in_specs=[outside] * 6,
        out_specs=whole,
        scratch_shapes=[
            vmem(K, 8, 128), pltpu.SMEM((K, K), F32), pltpu.SMEM((K,), F32), counts, counts, counts, dma(6),
            vmem(K, K, 8, 128), vmem(*field), vmem(10, 8, 128), vmem(*pair), vmem(*field),
            vmem(K, K, 8, 128), vmem(NTILES, K, K, 8, 128), vmem(2, K, K, 8, 128),
            *[vmem(*field) for _ in range(5)],
            *[vmem(*pair) for _ in range(8)], vmem(4, 8, 128),
            vmem(256, 128), vmem(256, 128), vmem(6, 8, 128), vmem(6, 8, 128), vmem(8, 128), vmem(8, 128),
            vmem(64, 128), vmem(64, 128), vmem(48, 128), vmem(48, 128), vmem(16, 128), vmem(16, 128),
            vmem(3, 128, 128), vmem(3, 128, 128), vmem(128, 128), vmem(2, 128, 128),
            vmem(1, 128), vmem(2, GX, 1, 128), vmem(2, GY, 1, 128), vmem(1, 128), vmem(GX * GY, 1, 128),
            dma(2, 8), dma(2, 8), dma(2, 8), dma(2, 8), dma(3), dma(3), dma(2), dma(2), dma(2), dma(2),
            pltpu.SemaphoreType.DMA, pltpu.SemaphoreType.DMA,
        ],
        compiler_params=pltpu.CompilerParams(collective_id=0, has_side_effects=True, vmem_limit_bytes=48 << 20),
    )(beta, design, prior, kept, removed, removed_labels)


def solution(mesh):
    placed = (
        P(None, "gx", "gy"),
        P(),
        P(),
        P(None, "gx", "gy"),
        P(None, "gx", "gy"),
        P(None, "gx", "gy"),
    )
    return jax.shard_map(
        local, mesh=mesh, in_specs=placed, out_specs=P(None, "gx", "gy"), check_vma=False
    )
```

```python
import jax
import jax.numpy as jnp
from jax import lax
from jax.experimental import pallas as pl
from jax.experimental.pallas import tpu as pltpu
from jax.sharding import PartitionSpec as P

K = 16
ITERS = 4
NTILES = 7
GX, GY = 8, 16
damping = 0.7
keep = 1.0 - damping
MESH = pl.DeviceIdType.MESH
F32 = jnp.float32

level_tiles = {0: (0, 1, 2), 1: (3, 4), 2: (5,), 3: (6,)}
tile_level = (0, 0, 0, 1, 1, 2, 3)
sideways = ((-1, -1), (-1, 1), (1, -1), (1, 1), (0, -1), (0, 1))
around = sideways + ((-1, 0), (1, 0))


def iota(axis):
    return lax.broadcasted_iota(jnp.int32, (8, 128), axis)


def take(x, index, axis):
    return jnp.take_along_axis(x, index, axis=axis, mode="promise_in_bounds")


def lroll(x, shift):
    return pltpu.roll(x, shift % 128, x.ndim - 1)


def sroll(x, shift):
    return pltpu.roll(x, shift % 8, x.ndim - 2)


def body(
    beta_in, design_in, prior_in, kept_in, removed_in, labels_in, out,
    beta, design, prior, kept, removed, labels, insem, dv, pv, mask, nat, wt, a, mi, mb,
    fb, d1, d2, rho, v,
    zs, qs, ss, ds, xs, rs, us, ws, scal,
    tw, tf, th, pw, pf, psw, psf, g1b, g2b, gs, s1w, s1f, ssw, ssf, s2w, s2f, r1w, r1f, rsw, rsf, r2w, r2f,
    lsend, lgx, lgy, lsum, lall,
    e0s, e0r, e1s, e1r, e2s, e2r, ags, agr, bgs, bgr, alls, allr,
):
    mx, my = lax.axis_index("gx"), lax.axis_index("gy")
    sub, lane = iota(0), iota(1)

    def device(dx, dy):
        return (lax.rem(mx + dx + GX, GX), lax.rem(my + dy + GY, GY))

    barrier = pltpu.get_barrier_semaphore()
    has = {-1: mx > 0, 1: mx < GX - 1}
    has_y = {-1: my > 0, 1: my < GY - 1}

    def exists(dx, dy):
        found = [table[d] for table, d in ((has, dx), (has_y, dy)) if d]
        return found[0] if len(found) == 1 else found[0] & found[1]

    def signal(dx, dy):
        pl.semaphore_signal(barrier, inc=1, device_id=device(dx, dy), device_id_type=MESH)

    corners = tuple(o for o in sideways if o[0] != 0)
    for dx, dy in corners:
        pl.when(exists(dx, dy))(lambda dx=dx, dy=dy: signal(dx, dy))
    greeted = [(0, d) for d in (1, 15, 4, 12, 8, 6, 10)] + [(d, 0) for d in range(1, GX)]
    for dx, dy in greeted:
        signal(dx, dy)
    beside_x = jnp.where((mx > 0) & (mx < GX - 1), 2, 1)
    beside_y = jnp.where((my > 0) & (my < GY - 1), 2, 1)
    peers = len(greeted) + beside_x * beside_y

    inputs = [
        pltpu.make_async_copy(src, dst, insem.at[i])
        for i, (src, dst) in enumerate(
            (
                (design_in, design), (prior_in, prior), (beta_in, beta),
                (kept_in, kept), (removed_in, removed), (labels_in, labels),
            )
        )
    ]
    for copy in inputs:
        copy.start()

    def clear(dx, dy):
        slot = sideways.index((dx, dy))
        for p in (pw, pf):
            p[slot] = jnp.zeros((32, 128), F32)

    for dx, dy in sideways:
        pl.when(~exists(dx, dy))(lambda dx=dx, dy=dy: clear(dx, dy))

    def clear_rows(i):
        for t in (tw, tf):
            t[pl.ds(128 + 64 * i, 64), :] = jnp.zeros((64, 128), F32)
        th[pl.ds(64 + 32 * i, 32), :] = jnp.zeros((32, 128), F32)

    pl.when(~has[1])(lambda: clear_rows(0))
    pl.when(~has[-1])(lambda: clear_rows(1))
    for r in (r1w, r1f, rsw, rsf):
        r[...] = jnp.zeros_like(r)

    def remote(src, dst, ssem, rsem, dx, dy):
        return pltpu.make_async_remote_copy(
            src_ref=src, dst_ref=dst, send_sem=ssem, recv_sem=rsem, device_id=device(dx, dy), device_id_type=MESH
        )

    def copies0(t, p, ps, k):
        out = []
        for j, (dx, dy) in enumerate(sideways):
            slot = sideways.index((-dx, -dy))
            out.append((remote(ps, p.at[slot], e0s.at[k, 2 + j], e0r.at[k, 2 + j], dx, dy), dx, dy))
        out.append((remote(t.at[pl.ds(0, 64)], t.at[pl.ds(128, 64)], e0s.at[k, 0], e0r.at[k, 0], -1, 0), -1, 0))
        out.append((remote(t.at[pl.ds(64, 64)], t.at[pl.ds(192, 64)], e0s.at[k, 1], e0r.at[k, 1], 1, 0), 1, 0))
        return out

    def start(copies):
        for copy, dx, dy in copies:
            pl.when(exists(dx, dy))(copy.start)

    def finish(copies):
        for copy, dx, dy in copies:
            pl.when(exists(-dx, -dy))(copy.wait_recv)
        for copy, dx, dy in copies:
            pl.when(exists(dx, dy))(copy.wait_send)

    def finish_all(copy):
        copy.wait_recv()
        copy.wait_send()

    group = (lane + 16) // 32 % 4
    right_side = lane % 32 < 16
    even_half = (lane < 32) | (lane >= 96)

    def pack(rows_of, ps):
        for q in range(4):
            total = rows_of(4 * q)
            for j in range(1, 4):
                total = jnp.where(group == j, lroll(rows_of(4 * q + j), 32 * j), total)
            ps[pl.ds(8 * q, 8), :] = total

    def load_main(t, dst):
        for c in range(K):
            dst[0, pl.ds(8 * c, 8), :] = t[pl.ds(c, 8, stride=32), :]
            dst[1, pl.ds(8 * c, 8), :] = t[pl.ds(16 + c, 8, stride=32), :]

    def load0(t, p, dst):
        load_main(t, dst)
        for q in range(4):
            rows = pl.ds(8 * q, 8)

            def merged(dx):
                return jnp.where(right_side, p[sideways.index((dx, 1)), rows, :], p[sideways.index((dx, -1)), rows, :])

            here, below, above = merged(0), merged(1), merged(-1)
            even = jnp.where(sub < 4, here, sroll(jnp.where(sub < 2, below, above), 4))
            odd = jnp.where(sub < 4, sroll(here, 4), jnp.where(sub < 6, below, above))
            for j in range(4):
                side = jnp.where(even_half, lroll(even, -32 * j), lroll(odd, 64 - 32 * j))
                dst[2, pl.ds(8 * (4 * q + j), 8), :] = side

    def natural_prepare(src, t, ps):
        pack(lambda c: jnp.concatenate([src[pl.ds(8 * c + i, 4, stride=2), :] for i in range(2)], axis=0), ps)
        for r in range(8):
            t[pl.ds(16 * r, 16), :] = src[pl.ds(r, 16, stride=8), :]

    def copies_again():
        out = []
        for i, dx in enumerate((-1, 1)):
            src, dst = tf.at[pl.ds(64 * i, 64)], tf.at[pl.ds(128 + 64 * i, 64)]
            out.append((remote(src, dst, e0s.at[2, i], e0r.at[2, i], dx, 0), dx, 0))
            src, dst = th.at[pl.ds(32 * i, 32)], th.at[pl.ds(64 + 32 * i, 32)]
            out.append((remote(src, dst, e0s.at[2, 2 + i], e0r.at[2, 2 + i], dx, 0), dx, 0))
        return out

    lane_even = lane % 2 == 0
    split = jnp.where(lane < 64, 2 * lane, 2 * (lane - 64) + 1)

    def restrict_pairs(src, first, g):
        for c in range(8):
            lo = src[first, pl.ds(8 * c, 8), :] + src[first + 1, pl.ds(8 * c, 8), :]
            hi = src[first, pl.ds(8 * c + 64, 8), :] + src[first + 1, pl.ds(8 * c + 64, 8), :]
            g[pl.ds(8 * c, 8), :] = take(jnp.where(lane_even, lo + lroll(lo, -1), hi + lroll(hi, 1)), split, 1)

    def copies1(s, sides, r, rsides, k):
        side_rows = {1: (0, 24, 40), -1: (8, 24, 16), 0: (8, 16, 0)}
        out = []
        for j, (dx, dy) in enumerate(sideways):
            first, size, target = side_rows[dx]
            slot = 0 if dy == 1 else 1
            src, dst = sides.at[slot, pl.ds(first, size)], rsides.at[slot, pl.ds(target, size)]
            out.append((remote(src, dst, e1s.at[k, j], e1r.at[k, j], dx, dy), dx, dy))
        for j, (dx, first, target) in enumerate(((-1, 8, 32), (1, 0, 88))):
            src, dst = s.at[pl.ds(first, 40)], r.at[pl.ds(target, 40)]
            out.append((remote(src, dst, e1s.at[k, 6 + j], e1r.at[k, 6 + j], dx, 0), dx, 0))
        return out

    middle = (lane >= 32) & (lane < 96)
    high = (lane // 32) % 2 == 1

    def start1(src, s, sides, r, rsides, k):
        restrict_pairs(src, 0, g1b)
        for c in range(4):
            first, second = g1b[pl.ds(8 * c, 8), :], lroll(g1b[pl.ds(8 * c + 32, 8), :], 32)
            gs[0, pl.ds(8 * c, 8), :] = jnp.where(high, first, second)
            gs[1, pl.ds(8 * c, 8), :] = jnp.where(high, second, first)
        for i in range(8):
            for slot in range(2):
                sides[slot, pl.ds(4 * i, 4), :] = gs[slot, pl.ds((i + 6) % 8, 4, stride=8), :]
        for i in range(6):
            s[pl.ds(8 * i, 8), :] = g1b[pl.ds((i + 7) % 8, 8, stride=8), :]
        start(copies1(s, sides, r, rsides, k))
        r[pl.ds(0, 32), :] = s[pl.ds(8, 32), :]

    def load1(r, rsides, dst):
        for tile, base in ((3, 0), (4, 1)):
            for c in range(4):
                left, right = (rsides[i, pl.ds(4 * base + c, 8, stride=8), :] for i in range(2))
                here = [r[pl.ds(8 * base + c + 4 * i, 8, stride=16), :] for i in range(2)]
                for j in range(4):
                    side = lroll(jnp.where(lane // 32 == j, right, left), 96 - 32 * j)
                    center = lroll(here[j % 2], 32 if j < 2 else 96)
                    dst[tile, pl.ds(8 * (c + 4 * j), 8), :] = jnp.where(middle, center, side)

    def copies2(s, r, k):
        return [
            remote(s, r.at[pl.ds(16 * (GX - d), 16)], e2s.at[k], e2r.at[k], d, 0) for d in range(1, GX)
        ]

    def finish2(r, k):
        rest = r.at[pl.ds(16, 16 * (GX - 1))]
        finish_all(remote(rest, rest, e2s.at[k], e2r.at[k], 1, 0))

    def start2(src, s, r, k):
        restrict_pairs(src, 3, g2b)
        s[pl.ds(0, 8), :] = g2b[pl.ds(0, 8, stride=8), :]
        s[pl.ds(8, 8), :] = g2b[pl.ds(1, 8, stride=8), :]
        for copy in copies2(s, r, k):
            copy.start()
        r[pl.ds(0, 16), :] = s[...]

    def load2(r, dst):
        for c in range(8):
            even, odd = r[pl.ds(c, 8, stride=16), :], r[pl.ds(8 + c, 8, stride=16), :]
            dst[5, pl.ds(8 * c, 8), :] = jnp.where(lane < 64, even, lroll(odd, 64))
            dst[5, pl.ds(8 * c + 64, 8), :] = jnp.where(lane < 64, lroll(even, 64), odd)

    twice = 2 * lane % 64

    def restrict3(src, dst):
        for c in range(K):
            x = src[5, pl.ds(8 * c, 8), :]
            x = x + lroll(x, 64)
            dst[6, pl.ds(8 * c, 8), :] = take(x + lroll(x, -1), twice, 1)

    def one(condition):
        return jnp.where(condition, 1.0, 0.0).astype(F32)

    for t in range(2):
        row = jnp.where(sub < 6, 2 * sub, 2 * sub - 16) + t
        at = 8 * mx + row
        mask[t] = one((at >= 0) & (at < 64))
    row = jnp.where(sub < 6, 2 * sub, 2 * sub - 16) + jnp.where(even_half, 0, 1)
    at = 8 * mx + row
    offset = (lane + 32) % 64 - 32
    column = 128 * my + jnp.where(offset < 0, offset, 128 + offset)
    mask[2] = one((at >= 0) & (at < 64) & (offset >= -16) & (offset < 16) & (column >= 0) & (column < 2048))
    for t in range(2):
        row = jnp.where(sub < 5, 2 * sub, 2 * sub - 16) + t
        at = 4 * mx + row
        column = lane - 32
        near = (row >= -5) & (row <= 8) & (column >= -26) & (column < 90)
        column = 64 * my + column
        mask[3 + t] = one(near & (at >= 0) & (at < 32) & (column >= 0) & (column < 1024))
    column = lane % 64 - 16
    near = (column >= -12) & (column < 44)
    column = 32 * my + column
    mask[5] = one(near & (column >= 0) & (column < 512))
    column = lane - 8
    near = (column >= -5) & (column < 21)
    column = 16 * my + column
    mask[6] = one(near & (column >= 0) & (column < 256))
    at = lax.rem(mx + sub, GX)
    first, last = at == 0, at == GX - 1
    mask[7] = one(~(((lane < 64) & first) | ((lane >= 64) & last)))
    mask[8] = one(~first)
    mask[9] = one(~last)

    for copy in inputs[:2]:
        copy.wait()

    def fill(j, carry):
        for k in range(K):
            dv[j, k] = jnp.full((8, 128), design[j, k], F32)
        return carry

    lax.fori_loop(0, K, fill, 0)

    for copy in inputs[2:]:
        copy.wait()
    logits = dv[:, 0] * beta[0]
    for k in range(1, K):
        logits = logits + dv[:, k] * beta[k]
    prob = 1.0 / (1.0 + jnp.exp(-logits))
    nat[0] = (kept[...].astype(F32) * prob * (1.0 - prob)).reshape(128, 128)
    nat[1] = (removed[...].astype(F32) * prob - labels[...].astype(F32)).reshape(128, 128)
    natural_prepare(nat.at[0], tw, psw)
    pl.semaphore_wait(barrier, peers)
    start(copies0(tw, pw, psw, 0))

    total = dv[0] * nat[1, pl.ds(0, 8), :]
    for j in range(1, K):
        total = total + dv[j] * nat[1, pl.ds(8 * j, 8), :]
    nat[1] = total.reshape(128, 128)
    natural_prepare(nat.at[1], tf, psf)
    start(copies0(tf, pf, psf, 1))

    for t in range(NTILES):
        for k in range(K):
            pv[t, pl.ds(8 * k, 8), :] = jnp.full((8, 128), prior[k] * 2.0 ** tile_level[t], F32)
    for ref in (zs, qs, ss, ds, xs, us, ws):
        ref[...] = jnp.zeros_like(ref)
    rest = jnp.zeros((4, 128), F32)
    for t in range(2):
        for c in range(K):
            rs[t, pl.ds(8 * c, 8), :] = jnp.concatenate([nat[1, pl.ds(8 * c + t, 4, stride=2), :], rest], axis=0)

    def weight(t, j):
        return jnp.where(mask[t] > 0.0, wt[t, pl.ds(pl.multiple_of(8 * j, 8), 8), :], 0.0)

    def invert(t, fine):
        w = [weight(t, j) for j in range(K)]
        for k in range(K):
            total = (dv[0, k] * w[0]) * dv[0, : k + 1]
            for j in range(1, K):
                total = total + (dv[j, k] * w[j]) * dv[j, : k + 1]
            a[k, : k + 1] = total
            a[k, k] = a[k, k] + 4.0 * pv[t, pl.ds(8 * k, 8), :]
            if fine:
                mb[t, k, : k + 1] = a[k, : k + 1]
                if k:
                    mb[t, :k, k] = a[k, :k]

        def line(i):
            if i == K - 1:
                return a[i, : i + 1]
            return jnp.concatenate([a[i, : i + 1], a[i + 1 :, i]], axis=0)

        def put(i, value):
            a[i, : i + 1] = value[: i + 1]
            if i < K - 1:
                a[i + 1 :, i] = value[i + 1 :]

        def replaced(value, i, entry):
            parts = [value[:i], entry[None], value[i + 1 :]]
            return jnp.concatenate([part for part in parts if part.shape[0]], axis=0)

        for p in range(0, K, 2):
            q = p + 1
            col1 = line(p)
            inv1 = 1.0 / col1[p]
            sc1 = col1 * inv1
            col2 = replaced(line(q) - sc1[q] * col1, p, sc1[q])
            inv2 = 1.0 / col2[q]
            sc2 = col2 * inv2
            for i in range(K):
                if i not in (p, q):
                    a[i, : i + 1] = a[i, : i + 1] - sc1[i] * col1[: i + 1] - sc2[i] * col2[: i + 1]
            line_p = replaced(sc1 - sc2[p] * col2, p, -inv1 - sc2[p] * col2[p])
            put(p, replaced(line_p, q, sc2[p]))
            put(q, replaced(sc2, q, -inv2))
        factor = -damping * mask[t]
        for i in range(K):
            value = a[i, : i + 1] * factor
            mi[t, i, : i + 1] = value
            if i:
                mi[t, :i, i] = value[:i]

    def invert_tiles(first, stop, fine=False):
        def step(t, carry):
            invert(t, fine)
            return carry

        lax.fori_loop(first, stop, step, 0)

    finish(copies0(tw, pw, psw, 0))
    load0(tw, pw, wt)
    start1(wt, s1w, ssw, r1w, rsw, 0)
    invert_tiles(0, 3, True)
    finish(copies0(tf, pf, psf, 1))
    load0(tf, pf, fb)

    def product(matrix, t, src):
        total = matrix[t, 0] * src[t, pl.ds(0, 8), :]
        for l in range(1, K):
            total = total + matrix[t, l] * src[t, pl.ds(8 * l, 8), :]
        return total.reshape(128, 128)

    STEP = 4

    def beside(level, src, g):
        def get(t):
            return src[t, pl.ds(8 * STEP * g, 8 * STEP), :].reshape(STEP, 8, 128)

        def pick(condition, x, y):
            return jnp.where(condition[None], x, y)

        if level == 0:
            e, o, h = get(0), get(1), get(2)
            y = lroll(h, 64)
            e1, o1, h1, y1 = lroll(e, 1), lroll(o, 1), lroll(h, 1), lroll(y, 1)
            em, om, hm, ym = lroll(e, -1), lroll(o, -1), lroll(h, -1), lroll(y, -1)
            start, end = lane == 0, lane == 127
            ne = o + sroll(o, 1) + pick(start, h1, e1) + pick(end, hm, em)
            no = e + sroll(e, -1) + pick(start, y1, o1) + pick(end, ym, om)
            nh = y + pick(even_half, sroll(y, 1), sroll(y, -1))
            nh = nh + pick(start, e1, pick(lane == 64, lroll(o1, 64), h1))
            nh = nh + pick(end, em, pick(lane == 63, lroll(om, 64), hm))
            return ne, no, nh
        if level == 1:
            e, o = get(3), get(4)
            ne = o + sroll(o, 1) + lroll(e, 1) + lroll(e, -1)
            no = e + sroll(e, -1) + lroll(o, 1) + lroll(o, -1)
            return ne, no
        if level == 2:
            x = get(5)
            y = lroll(x, 64)
            n = y + mask[7][None] * pick(lane < 64, sroll(y, 1), sroll(y, -1))
            return (n + lroll(x, 1) + lroll(x, -1),)
        x = get(6)
        return (mask[8][None] * sroll(x, 1) + mask[9][None] * sroll(x, -1) + lroll(x, 1) + lroll(x, -1),)

    def stencil(level, src, combine):
        for g in range(K // STEP):
            rows = pl.ds(8 * STEP * g, 8 * STEP)
            for t, n in zip(level_tiles[level], beside(level, src, g)):
                rho[t, rows, :] = combine(t, rows, pv[t, rows, :] * n.reshape(8 * STEP, 128))

    def descend(level):
        for t in level_tiles[level]:
            d1[t] = product(mi, t, fb)
        stencil(level, d1, lambda t, rows, n: keep * fb[t, rows, :] + n)
        for t in level_tiles[level]:
            value = product(mi, t, rho)
            d2[t] = value
            v[t] = d1[t] + value
        stencil(level, d2, lambda t, rows, n: keep * rho[t, rows, :] + n)

    def smooth(level, count):
        def step(i, carry):
            stencil(level, v, lambda t, rows, n: fb[t, rows, :] + n)
            for t in level_tiles[level]:
                v[t] = keep * v[t] + product(mi, t, rho)
            return carry

        for i in range(count):
            step(i, 0)

    up_rows = jnp.where(sub < 6, sub // 2, 7)
    up3 = lane % 64 // 2
    up2 = lane // 2 + 64 * (sub % 2)
    up1 = lane // 2 + 32
    up1_side = jnp.where(offset < 0, (offset + 32) // 2 + 16, offset // 2 + 96)
    sub_even = sub % 2 == 0

    def cycle(wait_first, wait_second, k):
        parity = lax.rem(k, 2)
        beside_now = rsf.at[parity]
        descend(0)
        start1(rho, s1f, ssf, r1f, beside_now, 1 + parity)
        wait_first()
        finish(copies1(s1f, ssf, r1f, beside_now, 1 + parity))
        load1(r1f, beside_now, fb)
        descend(1)
        start2(rho, s2f, r2f.at[parity], parity)
        wait_second()
        finish2(r2f.at[parity], parity)
        load2(r2f.at[parity], fb)
        descend(2)
        restrict3(rho, fb)
        v[6] = product(mi, 6, fb)
        smooth(3, 3)
        for c in range(K):
            rows = pl.ds(8 * c, 8)
            v[5, rows, :] = v[5, rows, :] + take(v[6, rows, :], up3, 1)
        smooth(2, 2)
        for c in range(K):
            rows = pl.ds(8 * c, 8)
            e = take(take(v[5, rows, :], up_rows, 0), up2, 1)
            for t in (3, 4):
                v[t, rows, :] = v[t, rows, :] + mask[t] * e
        smooth(1, 2)
        for c in range(K):
            rows = pl.ds(8 * c, 8)
            e = jnp.where(sub_even, take(v[3, rows, :], up_rows, 0), take(v[4, rows, :], up_rows, 0))
            main = take(e, up1, 1)
            v[0, rows, :] = v[0, rows, :] + main
            v[1, rows, :] = v[1, rows, :] + main
            v[2, rows, :] = v[2, rows, :] + take(e, up1_side, 1)
        smooth(0, 2)

    def copies_a(k):
        return [remote(lsend, lgx.at[k, GX - d], ags.at[k], agr.at[k], d, 0) for d in range(1, GX)]

    def copies_b(k):
        return [remote(lsum, lgy.at[k, GY - d], bgs.at[k], bgr.at[k], 0, d) for d in range(1, GY)]

    def finish_sum(landing, count, ssem, rsem):
        rest = landing.at[pl.ds(1, count - 1)]
        finish_all(remote(rest, rest, ssem, rsem, 0, 1))

    def dot(x, y):
        total = jnp.zeros((8, 128), F32)
        for t in range(2):
            for c in range(K):
                rows = pl.ds(8 * c, 8)
                total = total + x[t, rows, :] * y[t, rows, :]
        total = jnp.sum(jnp.where(sub < 4, total, 0.0), axis=0, keepdims=True)
        return jnp.sum(total, axis=1, keepdims=True)

    one_lane = lax.broadcasted_iota(jnp.int32, (1, 128), 1)

    def sum_parts():
        gamma, delta, cross = dot(rs, us), dot(ws, us), dot(ss, us)
        lsend[...] = jnp.where(one_lane == 0, gamma, jnp.where(one_lane == 1, delta, cross))

    def sum_start(k):
        sum_parts()
        for copy in copies_a(k):
            copy.start()
        lgx[k, 0] = lsend[...]

    def sum_turn(k):
        finish_sum(lgx.at[k], GX, ags.at[k], agr.at[k])
        total = lgx[k, 0]
        for i in range(1, GX):
            total = total + lgx[k, i]
        lsum[...] = total
        for copy in copies_b(k):
            copy.start()
        lgy[k, 0] = total

    def sum_finish(k, use_beta):
        finish_sum(lgy.at[k], GY, bgs.at[k], bgr.at[k])
        scalars(jnp.sum(lgy[k], axis=0), use_beta)

    def sum_at_once():
        sum_parts()
        for d in range(1, GX * GY):
            dx, dy = d // GY, d % GY
            slot = (GX - dx) % GX * GY + (GY - dy) % GY
            remote(lsend, lall.at[slot], alls, allr, dx, dy).start()
        lall[0] = lsend[...]
        finish_sum(lall, GX * GY, alls, allr)
        scalars(jnp.sum(lall[...], axis=0), 1.0)

    def scalars(total, use_beta):

        def lane_of(i):
            value = jnp.sum(jnp.where(one_lane == i, total, 0.0), axis=1, keepdims=True)
            return jnp.broadcast_to(value, (8, 128))

        gamma, delta, cross = lane_of(0), lane_of(1), lane_of(2)
        beta_now = use_beta * gamma / scal[2]
        product_now = delta + 2.0 * beta_now * cross + beta_now * beta_now * scal[3]
        scal[0] = gamma / product_now
        scal[1] = beta_now
        scal[2] = gamma
        scal[3] = product_now

    scal[0] = jnp.full((8, 128), -1.0, F32)
    scal[1] = jnp.zeros((8, 128), F32)
    scal[2] = jnp.ones((8, 128), F32)
    scal[3] = jnp.zeros((8, 128), F32)

    def trip(k, carry):
        @pl.when(k > 0)
        def _():
            finish(copies_again())
            load_main(tf, fb)
            for c in range(K):
                fb[2, pl.ds(8 * c, 8), :] = th[pl.ds(c, 8, stride=16), :]

        before = lax.rem(k + 1, 2)

        def turn():
            @pl.when(k > 0)
            def _():
                sum_turn(before)

            @pl.when(k == 0)
            def _():
                finish(copies1(s1w, ssw, r1w, rsw, 0))
                load1(r1w, rsw, wt)
                start2(wt, s2w, r2w, 2)
                invert_tiles(3, 5)

        def coarse():
            @pl.when(k == 0)
            def _():
                finish2(r2w, 2)
                load2(r2w, wt)
                restrict3(wt, wt)
                invert_tiles(5, 7)

            @pl.when(k > 0)
            def _():
                sum_finish(before, jnp.where(k > 1, 1.0, 0.0))

        cycle(turn, coarse, k)
        stencil(0, v, lambda t, rows, n: n)
        for t in range(3):
            d1[t] = product(mb, t, v) - rho[t]

        for t in range(3):
            for c in range(K):
                rows = pl.ds(8 * c, 8)
                z = d1[t, rows, :] + scal[1] * zs[t, rows, :]
                zs[t, rows, :] = z
                old = ws[t, rows, :]
                if t < 2:
                    ss[t, rows, :] = old + scal[1] * ss[t, rows, :]
                ws[t, rows, :] = old - scal[0] * z

        @pl.when(k < ITERS - 1)
        def _():
            for i in range(4):
                tf[pl.ds(32 * i, 16), :] = ws[0, pl.ds(i, 16, stride=8), :]
                tf[pl.ds(32 * i + 16, 16), :] = ws[1, pl.ds(i, 16, stride=8), :]
                th[pl.ds(16 * i, 16), :] = ws[2, pl.ds(i, 16, stride=8), :]
            start(copies_again())

        for t in range(2):
            for c in range(K):
                rows = pl.ds(8 * c, 8)
                q = v[t, rows, :] + scal[1] * qs[t, rows, :]
                qs[t, rows, :] = q
                old = us[t, rows, :]
                d = old + scal[1] * ds[t, rows, :]
                ds[t, rows, :] = d
                xs[t, rows, :] = xs[t, rows, :] + scal[0] * d
                rs[t, rows, :] = rs[t, rows, :] - scal[0] * ss[t, rows, :]
                us[t, rows, :] = old - scal[0] * q

        @pl.when(k < ITERS - 1)
        def _():
            sum_start(lax.rem(k, 2))

        return carry

    lax.fori_loop(0, ITERS, trip, 0)
    sum_at_once()
    for t in range(2):
        for c in range(K):
            rows = pl.ds(8 * c, 8)
            d = us[t, rows, :] + scal[1] * ds[t, rows, :]
            xs[t, rows, :] = xs[t, rows, :] + scal[0] * d
    for i in range(4):
        tf[pl.ds(32 * i, 16), :] = xs[0, pl.ds(i, 16, stride=8), :]
        tf[pl.ds(32 * i + 16, 16), :] = xs[1, pl.ds(i, 16, stride=8), :]
    for c in range(K):
        out[c] = tf[pl.ds(c, 8, stride=16), :]


def local(beta, design, prior, kept, removed, removed_labels):
    def vmem(*shape):
        return pltpu.VMEM(shape, F32)

    def dma(*shape):
        return pltpu.SemaphoreType.DMA(shape)

    whole = pl.BlockSpec(memory_space=pltpu.VMEM)
    outside = pl.BlockSpec(memory_space=pltpu.HBM)
    counts = pltpu.VMEM((K, 8, 128), jnp.int32)
    field = (NTILES, 128, 128)
    pair = (2, 128, 128)
    return pl.pallas_call(
        body,
        out_shape=jax.ShapeDtypeStruct(beta.shape, F32),
        in_specs=[outside] * 6,
        out_specs=whole,
        scratch_shapes=[
            vmem(K, 8, 128), pltpu.SMEM((K, K), F32), pltpu.SMEM((K,), F32), counts, counts, counts, dma(6),
            vmem(K, K, 8, 128), vmem(*field), vmem(10, 8, 128), vmem(*pair), vmem(*field),
            vmem(K, K, 8, 128), vmem(NTILES, K, K, 8, 128), vmem(3, K, K, 8, 128),
            *[vmem(*field) for _ in range(5)],
            *[vmem(3 if i in (0, 7) else 2, 128, 128) for i in range(8)], vmem(4, 8, 128),
            vmem(256, 128), vmem(256, 128), vmem(128, 128), vmem(6, 32, 128), vmem(6, 32, 128), vmem(32, 128), vmem(32, 128),
            vmem(64, 128), vmem(64, 128), vmem(2, 32, 128), vmem(48, 128), vmem(48, 128), vmem(2, 32, 128), vmem(2, 32, 128),
            vmem(16, 128), vmem(16, 128),
            vmem(128, 128), vmem(128, 128), vmem(2, 64, 128), vmem(2, 2, 64, 128), vmem(128, 128), vmem(2, 128, 128),
            vmem(1, 128), vmem(2, GX, 1, 128), vmem(2, GY, 1, 128), vmem(1, 128), vmem(GX * GY, 1, 128),
            dma(3, 8), dma(3, 8), dma(3, 8), dma(3, 8), dma(3), dma(3), dma(2), dma(2), dma(2), dma(2),
            pltpu.SemaphoreType.DMA, pltpu.SemaphoreType.DMA,
        ],
        compiler_params=pltpu.CompilerParams(collective_id=0, has_side_effects=True, vmem_limit_bytes=48 << 20),
    )(beta, design, prior, kept, removed, removed_labels)


def solution(mesh):
    placed = (
        P(None, "gx", "gy"),
        P(),
        P(),
        P(None, "gx", "gy"),
        P(None, "gx", "gy"),
        P(None, "gx", "gy"),
    )
    return jax.shard_map(
        local, mesh=mesh, in_specs=placed, out_specs=P(None, "gx", "gy"), check_vma=False
    )
```
